32 devices in a mesh: scan: 16 (over z, y, x), col: 2 (over core).
Axes of the slice: x: 2, y: 2, z: 4, core: 2. Of those that a mesh axis runs over, the one named last changes fastest.
Arguments:
- frames: float32 [256, 128, 2048], P('scan', None, 'col'), may hold values from -6 to 6
- depth_offset: int32 [128], replicated, may hold values from -64 to 64
- band_width: int32 [128], replicated, may hold values from 1 to 8
- edge_level: int32 [128, 2048], P(None, 'col'), may hold values from 1 to 16
Outputs:
- volume: float32 [256, 128, 2048], P('scan', None, 'col')
The draws below stay inside these ranges and needn't reach their ends.
All inputs are finite; a program needn't handle non-finite values.
Results may differ from the reference program's by a relative error of at most 0.0003.
Values sent between devices are 32-bit elements; how exact they have to be, the bound alone decides.
A program may use at most 128 MiB of HBM per device.

```python
import jax
import jax.numpy as jnp
from jax import lax

R = 128
C = 2048
BAND = 8
SWEEPS = 6
DIFFUSE = 6
W = 256
SHIFT = 64


def with_ends(values, rng, smallest, largest):
    index_at = [jax.random.randint(jax.random.fold_in(rng, axis), (), 0, length) for axis, length in enumerate(values.shape)]
    widest = values.shape.index(max(values.shape))
    beside = index_at[:widest] + [(index_at[widest] + 1) % values.shape[widest]] + index_at[widest + 1:]
    return values.at[tuple(index_at)].set(smallest).at[tuple(beside)].set(largest)


def level_of(key, dims, cuts, low, high):
    def one(axis_at, parts):
        heights = jax.random.uniform(jax.random.fold_in(jax.random.fold_in(key, 6), axis_at), (parts,), jnp.float32, low / len(cuts), high / len(cuts))
        return jnp.repeat(jnp.exp(heights), dims[axis_at] // parts).reshape((-1,) + (1,) * (len(dims) - axis_at - 1))

    gain = one(*cuts[0])
    for cut in cuts[1:]:
        gain = gain * one(*cut)
    return gain


def gaussian(key, extent, deviation, limit, cuts=(), kind=jnp.bfloat16):
    factor_of = level_of(key, extent, cuts, -0.22, 0.18) if cuts else 1.0
    drawn = jax.random.normal(key, extent, jnp.float32) * deviation * factor_of
    return jnp.minimum(jnp.maximum(drawn, -limit), limit).astype(kind)


def setup_inputs(seed: int = 0) -> dict:
    key_of = jax.random.split(jax.random.key(seed), 5)
    return {
        "frames": gaussian(key_of[0], (W, R, C), 1.0, 6.0, ((0, 16), (2, 2)), jnp.float32),
        "depth_offset": with_ends(jax.random.randint(key_of[1], (R,), 0 - SHIFT, SHIFT + 1), jax.random.fold_in(key_of[1], 1), 0 - SHIFT, SHIFT).astype(jnp.int32),
        "band_width": with_ends(jax.random.randint(key_of[2], (R,), 1, BAND + 1), jax.random.fold_in(key_of[2], 1), 1, BAND).astype(jnp.int32),
        "edge_level": with_ends(jax.random.randint(key_of[3], (R, C), 1, 17), jax.random.fold_in(key_of[3], 1), 1, 16).astype(jnp.int32),
    }


TEMPORAL_KAPPA = 1.0
STEP_SIZE = 0.24
LEVEL_SCALE = 16.0


def diffuse_once(field, kappa, live_mask):
    change = (field[1:] - field[:-1]) * (live_mask[1:] * live_mask[:-1])
    flux_out = change / (1.0 + (change * change) / (kappa * kappa))
    zero_row = jnp.zeros_like(flux_out[:1])
    return field + STEP_SIZE * (jnp.concatenate([flux_out, zero_row], 0) - jnp.concatenate([zero_row, flux_out], 0))


def reference(frames, depth_offset, band_width, edge_level):
    def one_row(row_index):
        plane_rows = lax.dynamic_index_in_dim(frames, row_index, 1, keepdims=False)
        live_mask = jnp.ones((W, 1), jnp.float32)
        for sweep_no in range(SWEEPS):
            plane_rows = diffuse_once(plane_rows, TEMPORAL_KAPPA, live_mask)
        wire_signal = jnp.concatenate([plane_rows[:-1] - plane_rows[1:], jnp.zeros_like(plane_rows[:1])], 0)
        row_offset = lax.dynamic_index_in_dim(depth_offset, row_index, 0, keepdims=False)
        row_width = lax.dynamic_index_in_dim(band_width, row_index, 0, keepdims=False)
        padded = jnp.pad(wire_signal, ((SHIFT + BAND, SHIFT), (0, 0)))
        summed = jnp.zeros_like(wire_signal)
        for lag_step in range(BAND):
            start_at = (SHIFT + BAND - lag_step - row_offset).astype(jnp.int32)
            pieces = lax.dynamic_slice_in_dim(padded, start_at, W, 0)
            summed = summed + jnp.where(lag_step < row_width, pieces, jnp.zeros_like(pieces))
        profile = summed / row_width.astype(jnp.float32)
        edge_scale = lax.dynamic_index_in_dim(edge_level, row_index, 0, keepdims=True).astype(jnp.float32) / LEVEL_SCALE
        for sweep_no in range(DIFFUSE):
            profile = diffuse_once(profile, edge_scale, live_mask)
        return profile

    stacked = lax.map(one_row, jnp.arange(R, dtype=jnp.int32))
    return jnp.transpose(stacked, (1, 0, 2))
```

```python
import functools

import jax
import jax.numpy as jnp
from jax import lax
from jax.experimental import pallas as pl
from jax.experimental.pallas import tpu as pltpu
from jax.sharding import PartitionSpec as P

SWEEPS = 6
DIFFUSE = 6
BAND = 8
TEMPORAL_KAPPA = 1.0
STEP_SIZE = 0.24
LEVEL_SCALE = 16.0
LANES = 128
ROWS = 8
LEAD = 4
CHUNKS = 4
FAR_LO = DIFFUSE + BAND - 1
FAR_HI = DIFFUSE + 1


def sweep_pass(src, dst, sweeps, inverse, cols):
    n_in, n_out = src.shape[0], dst.shape[0]
    lag = n_in - n_out
    lead = lag // 2 + 2 * sweeps - 1
    streams = len(cols)

    def advance(t, carry):
        held, flux, made = carry
        at = jnp.minimum(t, n_in - 1)
        new_held, new_flux, new_made = [], [], []
        for s, col in enumerate(cols):
            fresh = src[at, :, pl.ds(col, LANES)]
            for level in range(sweeps):
                k = s * sweeps + level
                b = fresh if level == 0 else made[k - 1]
                a = held[k]
                c = b - a
                cc = c * c if inverse is None else c * c * inverse[s]
                f = c / (1.0 + cc)
                new_made.append(a + STEP_SIZE * (f - flux[k]))
                new_held.append(b)
                new_flux.append(f)
        return tuple(new_held), tuple(new_flux), tuple(new_made)

    def warm(t, carry):
        return advance(t, carry)

    def work(t, carry):
        carry = advance(t + lead, carry)
        for s, col in enumerate(cols):
            dst[t, :, pl.ds(col, LANES)] = carry[2][s * sweeps + sweeps - 1]
        return carry

    start = tuple(src[0, :, pl.ds(col, LANES)] for col in cols for _ in range(sweeps))
    init = (start, start, start)
    carry = lax.fori_loop(0, lead, warm, init)
    lax.fori_loop(0, n_out, work, carry, unroll=2)


def column_groups(width):
    cols = list(range(0, width, LANES))
    return [cols[i : i + 2] for i in range(0, len(cols), 2)]


def smooth_kernel(where_ref, own, lo, hi, out, ext):
    frames, width = own.shape[0], own.shape[2]
    first = where_ref[1] == 0
    last = where_ref[1] == LEAD - 1
    for i in range(SWEEPS):
        ext[i] = jnp.where(first, own[SWEEPS - 1 - i], lo[i])
        ext[SWEEPS + frames + i] = jnp.where(last, own[frames - 1 - i], hi[i])

    def put(i, _):
        ext[SWEEPS + i] = own[i]
        return 0

    lax.fori_loop(0, frames, put, 0, unroll=8)
    for cols in column_groups(width):
        sweep_pass(ext, out, SWEEPS, None, cols)


def depth_kernel(where_ref, off_ref, bw_ref, far_lo, lo, own, hi, far_hi, edge, out, win, prof):
    frames, width = own.shape[0], own.shape[2]
    all_frames = frames * LEAD
    z = where_ref[1]
    row0 = (where_ref[0] * pl.num_programs(0) + pl.program_id(0)) * ROWS
    base = 0
    for part in (far_lo, lo, own, hi, far_hi):
        count = part.shape[0]
        if count < 16:
            for i in range(count):
                win[base + i] = part[i]
        else:

            def put(i, _, part=part, base=base):
                win[base + i] = part[i]
                return 0

            lax.fori_loop(0, count, put, 0, unroll=8)
        base += count
    origin = FAR_LO + frames - z * frames
    sub = lax.broadcasted_iota(jnp.int32, (ROWS, LANES), 0)
    offs = [off_ref[row0 + r] for r in range(ROWS)]
    bws = [bw_ref[row0 + r] for r in range(ROWS)]
    widths = jnp.full((ROWS, LANES), 1.0, jnp.float32)
    for r in range(ROWS):
        widths = jnp.where(sub == r, bws[r].astype(jnp.float32), widths)
    masks = [sub == r for r in range(ROWS)]

    def fill(d, _):
        depth = z * frames + d - DIFFUSE
        depth = jnp.where(depth < 0, -1 - depth, depth)
        depth = jnp.where(depth >= all_frames, 2 * all_frames - 1 - depth, depth)
        at_a, at_b = [], []
        for r in range(ROWS):
            at = depth - offs[r] + 1
            at_b.append(jnp.clip(at, 0, all_frames - 1) + origin)
            at_a.append(jnp.clip(at - bws[r], 0, all_frames - 1) + origin)
        for col in range(0, width, LANES):
            lanes = pl.ds(col, LANES)
            a = win[at_a[0], :, lanes]
            b = win[at_b[0], :, lanes]
            for r in range(1, ROWS):
                a = jnp.where(masks[r], win[at_a[r], :, lanes], a)
                b = jnp.where(masks[r], win[at_b[r], :, lanes], b)
            prof[d, :, lanes] = (a - b) / widths
        return 0

    lax.fori_loop(0, frames + 2 * DIFFUSE, fill, 0)
    for cols in column_groups(width):
        inverse = []
        for col in cols:
            level = edge[:, pl.ds(col, LANES)].astype(jnp.float32) / LEVEL_SCALE
            inverse.append(1.0 / (level * level))
        sweep_pass(prof, out, DIFFUSE, inverse, cols)


def smooth(where, own, lo, hi):
    frames, rows, width = own.shape

    def spec(count):
        return pl.BlockSpec((count, ROWS, width), lambda i, w: (0, i, 0))

    return pl.pallas_call(
        smooth_kernel,
        out_shape=jax.ShapeDtypeStruct(own.shape, own.dtype),
        grid_spec=pltpu.PrefetchScalarGridSpec(
            num_scalar_prefetch=1,
            grid=(rows // ROWS,),
            in_specs=[spec(frames), spec(SWEEPS), spec(SWEEPS)],
            out_specs=spec(frames),
            scratch_shapes=[pltpu.VMEM((frames + 2 * SWEEPS, ROWS, width), jnp.float32)],
        ),
        cost_estimate=pl.CostEstimate(
            flops=own.size * 100, bytes_accessed=own.size * 8, transcendentals=0
        ),
    )(where, own, lo, hi)


def depth(where, off, bw, far_lo, lo, own, hi, far_hi, edge, chunk):
    frames, rows, width = own.shape
    tiles = rows // ROWS

    def spec(count):
        return pl.BlockSpec((count, ROWS, width), lambda i, w, o, b: (0, i, 0))

    return pl.pallas_call(
        depth_kernel,
        out_shape=jax.ShapeDtypeStruct(own.shape, own.dtype),
        grid_spec=pltpu.PrefetchScalarGridSpec(
            num_scalar_prefetch=3,
            grid=(tiles,),
            in_specs=[
                spec(FAR_LO),
                spec(frames),
                spec(frames),
                spec(frames),
                spec(FAR_HI),
                pl.BlockSpec((ROWS, width), lambda i, w, o, b: (w[0] * tiles + i, chunk)),
            ],
            out_specs=spec(frames),
            scratch_shapes=[
                pltpu.VMEM((3 * frames + FAR_LO + FAR_HI, ROWS, width), jnp.float32),
                pltpu.VMEM((frames + 2 * DIFFUSE, ROWS, width), jnp.float32),
            ],
        ),
        cost_estimate=pl.CostEstimate(
            flops=own.size * 150, bytes_accessed=own.size * 20, transcendentals=0
        ),
    )(where, off, bw, far_lo, lo, own, hi, far_hi, edge)


def body(frames, depth_offset, band_width, edge_level):
    scan = lax.axis_size("scan")
    group = scan // LEAD
    me = lax.axis_index("scan")
    where = jnp.stack([me % group, me // group]).astype(jnp.int32)
    groups = [[z * group + k for k in range(group)] for z in range(LEAD)]
    cols = frames.shape[2]
    width = max(LANES, cols // CHUNKS)

    def move(value, step):
        pairs = [(i, i + step * group) for i in range(scan) if 0 <= i + step * group < scan]
        return lax.ppermute(value, "scan", pairs)

    pieces = []
    for chunk in range(cols // width):
        part = lax.slice_in_dim(frames, chunk * width, (chunk + 1) * width, axis=2)
        own = lax.all_to_all(
            part, "scan", split_axis=1, concat_axis=0, tiled=True, axis_index_groups=groups
        )
        lo = move(own[-SWEEPS:], 1)
        hi = move(own[:SWEEPS], -1)
        own = smooth(where, own, lo, hi)
        below = move(own, 1)
        above = move(own, -1)
        far_lo = move(own[-FAR_LO:], 2)
        far_hi = move(own[:FAR_HI], -2)
        made = depth(
            where, depth_offset, band_width, far_lo, below, own, above, far_hi, edge_level, chunk
        )
        made = lax.all_to_all(
            made, "scan", split_axis=0, concat_axis=1, tiled=True, axis_index_groups=groups
        )
        pieces.append(made)
    return jnp.concatenate(pieces, axis=2)


def solution(mesh):
    placed = (P("scan", None, "col"), P(), P(), P(None, "col"))
    return jax.shard_map(
        body, mesh=mesh, in_specs=placed, out_specs=P("scan", None, "col"), check_vma=False
    )
```

```python
import functools

import jax
import jax.numpy as jnp
from jax import lax
from jax.experimental import pallas as pl
from jax.experimental.pallas import tpu as pltpu
from jax.sharding import PartitionSpec as P

SWEEPS = 6
DIFFUSE = 6
BAND = 8
STEP_SIZE = 0.24
LEVEL_SCALE = 16.0
LANES = 128
ROWS = 8
LEAD = 4
FAR_LO = DIFFUSE + BAND - 1
FAR_HI = DIFFUSE + 1
MESH = pl.DeviceIdType.MESH


def sweep_pass(src, dst, dst_from, n_in, n_out, sweeps, inverse, tiles):
    lead = (n_in - n_out) // 2 + 2 * sweeps - 1

    def advance(t, carry):
        held, flux, made = carry
        at = jnp.minimum(t, n_in - 1)
        new_held, new_flux, new_made = [], [], []
        for s, tile in enumerate(tiles):
            fresh = src[at, tile, :]
            for level in range(sweeps):
                k = s * sweeps + level
                b = fresh if level == 0 else made[k - 1]
                a = held[k]
                c = b - a
                cc = c * c if inverse is None else c * c * inverse[s]
                f = c / (1.0 + cc)
                new_made.append(a + STEP_SIZE * (f - flux[k]))
                new_held.append(b)
                new_flux.append(f)
        return tuple(new_held), tuple(new_flux), tuple(new_made)

    def work(t, carry):
        carry = advance(t + lead, carry)
        for s, tile in enumerate(tiles):
            dst[dst_from + t, tile, :] = carry[2][s * sweeps + sweeps - 1]
        return carry

    start = tuple(src[0, tile, :] for tile in tiles for _ in range(sweeps))
    carry = lax.fori_loop(0, lead, advance, (start, start, start))
    lax.fori_loop(0, n_out, work, carry)


def kernel(group, chunks, off_ref, bw_ref, x, edge, out, *scratch):
    wins = scratch[:chunks]
    (raw, made, prof, edge_v, in_send, in_recv, in_own, halo_send, halo_recv,
     far_send, far_recv, out_send, out_recv, out_own, edge_sem) = scratch[chunks:]
    local = x.shape[0]
    rows = x.shape[1] // group
    frames = local * group
    all_frames = frames * LEAD
    own_at = FAR_LO + frames
    me = lax.axis_index("scan")
    k = lax.rem(me, group)
    z = lax.div(me, group)
    tile_count = rows // ROWS
    pair = 2 if tile_count % 2 == 0 else 1

    def rows_of(j):
        return pl.ds(pl.multiple_of(j * rows, ROWS), rows)

    def cols_of(c):
        return pl.ds(c * LANES, LANES)

    def mate(m):
        return z * group + lax.rem(k + m, group)

    has = {1: z < LEAD - 1, -1: z > 0, 2: z < LEAD - 2, -2: z > 1}

    barrier = pltpu.get_barrier_semaphore()
    for m in range(1, group):
        pl.semaphore_signal(barrier, inc=1, device_id={"scan": mate(m)}, device_id_type=MESH)
    for step, there in has.items():

        @pl.when(there)
        def _(step=step):
            pl.semaphore_signal(
                barrier, inc=1, device_id={"scan": me + step * group}, device_id_type=MESH
            )

    count = group - 1
    for there in has.values():
        count = count + there.astype(jnp.int32)
    pl.semaphore_wait(barrier, count)

    def in_copy(c, m):
        return pltpu.make_async_remote_copy(
            src_ref=x.at[:, rows_of(lax.rem(k + m, group)), cols_of(c)],
            dst_ref=raw.at[c, pl.ds(SWEEPS + k * local, local)],
            send_sem=in_send.at[c, m - 1],
            recv_sem=in_recv.at[c, m - 1],
            device_id={"scan": mate(m)},
            device_id_type=MESH,
        )

    def in_local(c):
        return pltpu.make_async_copy(
            x.at[:, rows_of(k), cols_of(c)],
            raw.at[c, pl.ds(SWEEPS + k * local, local)],
            in_own.at[c],
        )

    def out_copy(c, m):
        return pltpu.make_async_remote_copy(
            src_ref=made.at[c, pl.ds(lax.rem(k + m, group) * local, local)],
            dst_ref=out.at[:, rows_of(k), cols_of(c)],
            send_sem=out_send.at[c, m - 1],
            recv_sem=out_recv.at[c, m - 1],
            device_id={"scan": mate(m)},
            device_id_type=MESH,
        )

    def out_local(c):
        return pltpu.make_async_copy(
            made.at[c, pl.ds(k * local, local)],
            out.at[:, rows_of(k), cols_of(c)],
            out_own.at[c],
        )

    def z_copy(src, dst, sems, c, i, step):
        send, recv = sems
        return pltpu.make_async_remote_copy(
            src_ref=src,
            dst_ref=dst,
            send_sem=send.at[c, i],
            recv_sem=recv.at[c, i],
            device_id={"scan": me + step * group},
            device_id_type=MESH,
        )

    def halo_copies(c):
        sems = (halo_send, halo_recv)
        up = z_copy(raw.at[c, pl.ds(frames, SWEEPS)], raw.at[c, pl.ds(0, SWEEPS)], sems, c, 0, 1)
        down = z_copy(
            raw.at[c, pl.ds(SWEEPS, SWEEPS)],
            raw.at[c, pl.ds(SWEEPS + frames, SWEEPS)], sems, c, 1, -1,
        )
        return ((1, up), (-1, down))

    def far_copies(c):
        win, sems = wins[c], (far_send, far_recv)
        own = win.at[pl.ds(own_at, frames)]
        return (
            (1, z_copy(own, win.at[pl.ds(FAR_LO, frames)], sems, c, 0, 1)),
            (-1, z_copy(own, win.at[pl.ds(own_at + frames, frames)], sems, c, 1, -1)),
            (2, z_copy(win.at[pl.ds(own_at + frames - FAR_LO, FAR_LO)],
                       win.at[pl.ds(0, FAR_LO)], sems, c, 2, 2)),
            (-2, z_copy(win.at[pl.ds(own_at, FAR_HI)],
                        win.at[pl.ds(own_at + 2 * frames, FAR_HI)], sems, c, 3, -2)),
        )

    def start(copies):
        for step, copy in copies:
            pl.when(has[step])(copy.start)

    def wait_recv(copies):
        for step, copy in copies:
            pl.when(has[-step])(copy.wait_recv)

    def wait_send(copies):
        for step, copy in copies:
            pl.when(has[step])(copy.wait_send)

    edge_copy = pltpu.make_async_copy(edge.at[rows_of(k)], edge_v, edge_sem)
    for c in range(chunks):
        in_local(c).start()
        for m in range(1, group):
            in_copy(c, m).start()
    edge_copy.start()

    def arrive(c):
        in_local(c).wait()
        for m in range(1, group):
            in_copy(c, m).wait_recv()
        start(halo_copies(c))

    def smooth(c):
        wait_recv(halo_copies(c))

        @pl.when(z == 0)
        def _():
            for i in range(SWEEPS):
                raw[c, i] = raw[c, 2 * SWEEPS - 1 - i]

        @pl.when(z == LEAD - 1)
        def _():
            for i in range(SWEEPS):
                raw[c, SWEEPS + frames + i] = raw[c, SWEEPS + frames - 1 - i]

        def one(p, _):
            tiles = [pl.ds(pl.multiple_of((p * pair + s) * ROWS, ROWS), ROWS) for s in range(pair)]
            sweep_pass(
                raw.at[c], wins[c], own_at, frames + 2 * SWEEPS, frames, SWEEPS, None, tiles
            )
            return 0

        lax.fori_loop(0, tile_count // pair, one, 0)
        start(far_copies(c))

    def repeat(win, first, count, source):
        def one(i, _):
            win[first + i] = win[source]
            return 0

        lax.fori_loop(0, count, one, 0)

    def depth(c):
        win = wins[c]
        wait_recv(far_copies(c))
        pl.when(z == 0)(lambda: repeat(win, 0, own_at, own_at))
        pl.when(z == 1)(lambda: repeat(win, 0, FAR_LO, FAR_LO))
        end = own_at + frames
        pl.when(z == LEAD - 1)(lambda: repeat(win, end, frames + FAR_HI, end - 1))
        pl.when(z == LEAD - 2)(lambda: repeat(win, end + frames, FAR_HI, end + frames - 1))
        sub = lax.broadcasted_iota(jnp.int32, (ROWS, LANES), 0)

        def one_tile(p, _):
            tile = pl.ds(pl.multiple_of(p * ROWS, ROWS), ROWS)
            row0 = k * rows + p * ROWS
            at_b = [own_at - z * frames + 1 - off_ref[row0 + r] for r in range(ROWS)]
            bws = [bw_ref[row0 + r] for r in range(ROWS)]
            at_a = [at_b[r] - bws[r] for r in range(ROWS)]
            widths = jnp.where(sub == 0, bws[0].astype(jnp.float32), 1.0)
            for r in range(1, ROWS):
                widths = jnp.where(sub == r, bws[r].astype(jnp.float32), widths)

            def fill(d, _):
                at = z * frames + d - DIFFUSE
                at = jnp.where(at < 0, -1 - at, at)
                at = jnp.where(at >= all_frames, 2 * all_frames - 1 - at, at)
                a = win[at + at_a[0], tile, :]
                b = win[at + at_b[0], tile, :]
                for r in range(1, ROWS):
                    a = jnp.where(sub == r, win[at + at_a[r], tile, :], a)
                    b = jnp.where(sub == r, win[at + at_b[r], tile, :], b)
                prof[d, tile, :] = (a - b) / widths
                return 0

            lax.fori_loop(0, frames + 2 * DIFFUSE, fill, 0)
            return 0

        lax.fori_loop(0, tile_count, one_tile, 0)

        def one(p, _):
            tiles = [pl.ds(pl.multiple_of((p * pair + s) * ROWS, ROWS), ROWS) for s in range(pair)]
            inverse = []
            for tile in tiles:
                level = edge_v[tile, pl.ds(c * LANES, LANES)].astype(jnp.float32) / LEVEL_SCALE
                inverse.append(1.0 / (level * level))
            sweep_pass(
                prof, made.at[c], 0, frames + 2 * DIFFUSE, frames, DIFFUSE, inverse, tiles
            )
            return 0

        lax.fori_loop(0, tile_count // pair, one, 0)
        out_local(c).start()
        for m in range(1, group):
            out_copy(c, m).start()

    arrive(0)
    for c in range(chunks):
        if c + 1 < chunks:
            arrive(c + 1)
        smooth(c)
        if c == 0:
            edge_copy.wait()
        else:
            depth(c - 1)
    depth(chunks - 1)
    for c in range(chunks):
        for m in range(1, group):
            in_copy(c, m).wait_send()
        wait_send(halo_copies(c))
        wait_send(far_copies(c))
        out_local(c).wait()
        for m in range(1, group):
            out_copy(c, m).wait()


def body(frames, depth_offset, band_width, edge_level):
    group = lax.axis_size("scan") // LEAD
    local, all_rows, cols = frames.shape
    chunks, rows, block = cols // LANES, all_rows // group, local * group
    dma = pltpu.SemaphoreType.DMA
    smem = pl.BlockSpec(memory_space=pltpu.SMEM)
    anywhere = pl.BlockSpec(memory_space=pl.ANY)
    win = pltpu.VMEM((3 * block + FAR_LO + FAR_HI, rows, LANES), jnp.float32)
    return pl.pallas_call(
        functools.partial(kernel, group, chunks),
        out_shape=jax.ShapeDtypeStruct(frames.shape, frames.dtype),
        in_specs=[smem, smem, anywhere, anywhere],
        out_specs=anywhere,
        scratch_shapes=[win] * chunks
        + [
            pltpu.VMEM((chunks, block + 2 * SWEEPS, rows, LANES), jnp.float32),
            pltpu.VMEM((chunks, block, rows, LANES), jnp.float32),
            pltpu.VMEM((block + 2 * DIFFUSE, rows, LANES), jnp.float32),
            pltpu.VMEM((rows, cols), jnp.int32),
            dma((chunks, group - 1)),
            dma((chunks, group - 1)),
            dma((chunks,)),
            dma((chunks, 2)),
            dma((chunks, 2)),
            dma((chunks, 4)),
            dma((chunks, 4)),
            dma((chunks, group - 1)),
            dma((chunks, group - 1)),
            dma((chunks,)),
            dma,
        ],
        compiler_params=pltpu.CompilerParams(
            collective_id=0, has_side_effects=True, vmem_limit_bytes=60 * 1024 * 1024
        ),
    )(depth_offset, band_width, frames, edge_level)


def solution(mesh):
    placed = (P("scan", None, "col"), P(), P(), P(None, "col"))
    return jax.shard_map(
        body, mesh=mesh, in_specs=placed, out_specs=P("scan", None, "col"), check_vma=False
    )
```

```python
import functools

import jax
import jax.numpy as jnp
from jax import lax
from jax.experimental import pallas as pl
from jax.experimental.pallas import tpu as pltpu
from jax.sharding import PartitionSpec as P

SWEEPS = 6
DIFFUSE = 6
BAND = 8
STEP_SIZE = 0.24
LEVEL_SCALE = 16.0
LANES = 128
ROWS = 8
LEAD = 4
FAR_LO = DIFFUSE + BAND - 1
FAR_HI = DIFFUSE + 1
LAG = 2
MESH = pl.DeviceIdType.MESH


def sweep_pass(src, dst, dst_from, n_in, n_out, sweeps, inverse, tiles):
    lead = (n_in - n_out) // 2 + 2 * sweeps - 1

    def advance(t, carry):
        held, flux, made = carry
        at = jnp.minimum(t, n_in - 1)
        new_held, new_flux, new_made = [], [], []
        for s, tile in enumerate(tiles):
            fresh = src[at, tile, :]
            for level in range(sweeps):
                k = s * sweeps + level
                b = fresh if level == 0 else made[k - 1]
                a = held[k]
                c = b - a
                cc = c * c if inverse is None else c * c * inverse[s]
                d = 1.0 + cc
                q = pl.reciprocal(d, approx=True)
                f = c * (q * (2.0 - d * q))
                new_made.append(a + STEP_SIZE * (f - flux[k]))
                new_held.append(b)
                new_flux.append(f)
        return tuple(new_held), tuple(new_flux), tuple(new_made)

    def work(t, carry):
        carry = advance(t + lead, carry)
        for s, tile in enumerate(tiles):
            dst[dst_from + t, tile, :] = carry[2][s * sweeps + sweeps - 1]
        return carry

    start = tuple(src[0, tile, :] for tile in tiles for _ in range(sweeps))
    carry = lax.fori_loop(0, lead, advance, (start, start, start))
    lax.fori_loop(0, n_out, work, carry, unroll=2)


def kernel(group, chunks, off_ref, bw_ref, x, edge, out, *scratch):
    wins = scratch[:chunks]
    (raw, made, prof, edge_v, in_send, in_recv, in_own, halo_send, halo_recv,
     far_send, far_recv, out_send, out_recv, out_own, edge_sem) = scratch[chunks:]
    local = x.shape[0]
    rows = x.shape[1] // group
    frames = local * group
    all_frames = frames * LEAD
    own_at = FAR_LO + frames
    me = lax.axis_index("scan")
    k = lax.rem(me, group)
    z = lax.div(me, group)
    tile_count = rows // ROWS
    pair = 2 if tile_count % 2 == 0 else 1

    def rows_of(j):
        return pl.ds(pl.multiple_of(j * rows, ROWS), rows)

    def cols_of(c):
        return pl.ds(c * LANES, LANES)

    def mate(m):
        return z * group + lax.rem(k + m, group)

    inner = jnp.logical_and(z > 0, z < LEAD - 1)
    has = {1: z < LEAD - 1, -1: z > 0, 2: inner, -2: inner}
    gets = {1: z > 0, -1: z < LEAD - 1, 2: z > 1, -2: z < LEAD - 2}

    barrier = pltpu.get_barrier_semaphore()
    for m in range(1, group):
        pl.semaphore_signal(barrier, inc=1, device_id={"scan": mate(m)}, device_id_type=MESH)
    for step in (1, -1):

        @pl.when(has[step])
        def _(step=step):
            pl.semaphore_signal(
                barrier, inc=1, device_id={"scan": me + step * group}, device_id_type=MESH
            )

    count = group - 1
    for step in (1, -1):
        count = count + has[step].astype(jnp.int32)
    pl.semaphore_wait(barrier, count)

    def in_copy(c, m):
        return pltpu.make_async_remote_copy(
            src_ref=x.at[:, rows_of(lax.rem(k + m, group)), cols_of(c)],
            dst_ref=raw.at[c, pl.ds(SWEEPS + k * local, local)],
            send_sem=in_send.at[c, m - 1],
            recv_sem=in_recv.at[c, m - 1],
            device_id={"scan": mate(m)},
            device_id_type=MESH,
        )

    def in_local(c):
        return pltpu.make_async_copy(
            x.at[:, rows_of(k), cols_of(c)],
            raw.at[c, pl.ds(SWEEPS + k * local, local)],
            in_own.at[c],
        )

    def out_copy(c, m):
        return pltpu.make_async_remote_copy(
            src_ref=made.at[c, pl.ds(lax.rem(k + m, group) * local, local)],
            dst_ref=out.at[:, rows_of(k), cols_of(c)],
            send_sem=out_send.at[c, m - 1],
            recv_sem=out_recv.at[c, m - 1],
            device_id={"scan": mate(m)},
            device_id_type=MESH,
        )

    def out_local(c):
        return pltpu.make_async_copy(
            made.at[c, pl.ds(k * local, local)],
            out.at[:, rows_of(k), cols_of(c)],
            out_own.at[c],
        )

    def z_copy(src, dst, sems, c, i, step):
        send, recv = sems
        return pltpu.make_async_remote_copy(
            src_ref=src,
            dst_ref=dst,
            send_sem=send.at[c, i],
            recv_sem=recv.at[c, i],
            device_id={"scan": me + step * group},
            device_id_type=MESH,
        )

    def halo_copies(c):
        sems = (halo_send, halo_recv)
        up = z_copy(raw.at[c, pl.ds(frames, SWEEPS)], raw.at[c, pl.ds(0, SWEEPS)], sems, c, 0, 1)
        down = z_copy(
            raw.at[c, pl.ds(SWEEPS, SWEEPS)],
            raw.at[c, pl.ds(SWEEPS + frames, SWEEPS)], sems, c, 1, -1,
        )
        return ((1, up), (-1, down))

    def near_copies(c, first):
        win, end = wins[c], own_at + frames

        def one(src, dst, count, i, step):
            return z_copy(
                win.at[pl.ds(src, count)], win.at[pl.ds(dst, count)], (far_send, far_recv), c, i, step
            )

        if first:
            return (
                (1, one(end - FAR_LO, own_at - FAR_LO, FAR_LO, 0, 1)),
                (-1, one(own_at, end, FAR_HI, 1, -1)),
            )
        return (
            (1, one(own_at, FAR_LO, frames - FAR_LO, 2, 1)),
            (-1, one(own_at + FAR_HI, end + FAR_HI, frames - FAR_HI, 3, -1)),
        )

    def far_copies(c):
        win, end = wins[c], own_at + frames
        sems = (far_send, far_recv)
        up = z_copy(win.at[pl.ds(own_at - FAR_LO, FAR_LO)], win.at[pl.ds(0, FAR_LO)], sems, c, 4, 1)
        down = z_copy(
            win.at[pl.ds(end, FAR_HI)], win.at[pl.ds(end + frames, FAR_HI)], sems, c, 5, -1
        )
        return ((2, up), (-2, down))

    def start(copies):
        for step, copy in copies:
            pl.when(has[step])(copy.start)

    def wait_recv(copies):
        for step, copy in copies:
            pl.when(gets[step])(copy.wait_recv)

    def wait_send(copies):
        for step, copy in copies:
            pl.when(has[step])(copy.wait_send)

    edge_copy = pltpu.make_async_copy(edge.at[rows_of(k)], edge_v, edge_sem)
    for c in range(chunks):
        in_local(c).start()
        for m in range(1, group):
            in_copy(c, m).start()
    edge_copy.start()

    def arrive(c):
        in_local(c).wait()
        for m in range(1, group):
            in_copy(c, m).wait_recv()
        start(halo_copies(c))

    def smooth(c):
        wait_recv(halo_copies(c))

        @pl.when(z == 0)
        def _():
            for i in range(SWEEPS):
                raw[c, i] = raw[c, 2 * SWEEPS - 1 - i]

        @pl.when(z == LEAD - 1)
        def _():
            for i in range(SWEEPS):
                raw[c, SWEEPS + frames + i] = raw[c, SWEEPS + frames - 1 - i]

        def one(p, _):
            tiles = [pl.ds(pl.multiple_of((p * pair + s) * ROWS, ROWS), ROWS) for s in range(pair)]
            sweep_pass(
                raw.at[c], wins[c], own_at, frames + 2 * SWEEPS, frames, SWEEPS, None, tiles
            )
            return 0

        lax.fori_loop(0, tile_count // pair, one, 0)
        start(near_copies(c, True))
        start(near_copies(c, False))

    def forward(c):
        wait_recv(near_copies(c, True))
        start(far_copies(c))

    def repeat(win, first, count, source):
        def one(i, _):
            win[first + i] = win[source]
            return 0

        lax.fori_loop(0, count, one, 0)

    def depth(c):
        win = wins[c]
        wait_recv(near_copies(c, False))
        wait_recv(far_copies(c))
        pl.when(z == 0)(lambda: repeat(win, 0, own_at, own_at))
        pl.when(z == 1)(lambda: repeat(win, 0, FAR_LO, FAR_LO))
        end = own_at + frames
        pl.when(z == LEAD - 1)(lambda: repeat(win, end, frames + FAR_HI, end - 1))
        pl.when(z == LEAD - 2)(lambda: repeat(win, end + frames, FAR_HI, end + frames - 1))
        sub = lax.broadcasted_iota(jnp.int32, (ROWS, LANES), 0)

        def one_tile(p, _):
            tile = pl.ds(pl.multiple_of(p * ROWS, ROWS), ROWS)
            row0 = k * rows + p * ROWS
            at_b = [own_at - z * frames + 1 - off_ref[row0 + r] for r in range(ROWS)]
            bws = [bw_ref[row0 + r] for r in range(ROWS)]
            at_a = [at_b[r] - bws[r] for r in range(ROWS)]
            widths = jnp.where(sub == 0, bws[0].astype(jnp.float32), 1.0)
            for r in range(1, ROWS):
                widths = jnp.where(sub == r, bws[r].astype(jnp.float32), widths)

            def fill(d, _):
                at = z * frames + d - DIFFUSE
                at = jnp.where(at < 0, -1 - at, at)
                at = jnp.where(at >= all_frames, 2 * all_frames - 1 - at, at)
                a = win[at + at_a[0], tile, :]
                b = win[at + at_b[0], tile, :]
                for r in range(1, ROWS):
                    a = jnp.where(sub == r, win[at + at_a[r], tile, :], a)
                    b = jnp.where(sub == r, win[at + at_b[r], tile, :], b)
                prof[d, tile, :] = (a - b) / widths
                return 0

            lax.fori_loop(0, frames + 2 * DIFFUSE, fill, 0, unroll=4)
            return 0

        lax.fori_loop(0, tile_count, one_tile, 0)

        def one(p, _):
            tiles = [pl.ds(pl.multiple_of((p * pair + s) * ROWS, ROWS), ROWS) for s in range(pair)]
            inverse = []
            for tile in tiles:
                level = edge_v[tile, pl.ds(c * LANES, LANES)].astype(jnp.float32) / LEVEL_SCALE
                inverse.append(1.0 / (level * level))
            sweep_pass(
                prof, made.at[c], 0, frames + 2 * DIFFUSE, frames, DIFFUSE, inverse, tiles
            )
            return 0

        lax.fori_loop(0, tile_count // pair, one, 0)
        out_local(c).start()
        for m in range(1, group):
            out_copy(c, m).start()

    arrive(0)
    for c in range(chunks):
        if c + 1 < chunks:
            arrive(c + 1)
        if c >= 1:
            forward(c - 1)
        smooth(c)
        if c == 0:
            edge_copy.wait()
        if c >= LAG:
            depth(c - LAG)
    for c in range(max(chunks - LAG, 0), chunks):
        if c == chunks - 1:
            forward(c)
        depth(c)
    for c in range(chunks):
        for m in range(1, group):
            in_copy(c, m).wait_send()
        wait_send(halo_copies(c))
        wait_send(near_copies(c, True))
        wait_send(near_copies(c, False))
        wait_send(far_copies(c))
        out_local(c).wait()
        for m in range(1, group):
            out_copy(c, m).wait()


def body(frames, depth_offset, band_width, edge_level):
    group = lax.axis_size("scan") // LEAD
    local, all_rows, cols = frames.shape
    chunks, rows, block = cols // LANES, all_rows // group, local * group
    dma = pltpu.SemaphoreType.DMA
    smem = pl.BlockSpec(memory_space=pltpu.SMEM)
    anywhere = pl.BlockSpec(memory_space=pl.ANY)
    win = pltpu.VMEM((3 * block + FAR_LO + FAR_HI, rows, LANES), jnp.float32)
    return pl.pallas_call(
        functools.partial(kernel, group, chunks),
        out_shape=jax.ShapeDtypeStruct(frames.shape, frames.dtype),
        in_specs=[smem, smem, anywhere, anywhere],
        out_specs=anywhere,
        scratch_shapes=[win] * chunks
        + [
            pltpu.VMEM((chunks, block + 2 * SWEEPS, rows, LANES), jnp.float32),
            pltpu.VMEM((chunks, block, rows, LANES), jnp.float32),
            pltpu.VMEM((block + 2 * DIFFUSE, rows, LANES), jnp.float32),
            pltpu.VMEM((rows, cols), jnp.int32),
            dma((chunks, group - 1)),
            dma((chunks, group - 1)),
            dma((chunks,)),
            dma((chunks, 2)),
            dma((chunks, 2)),
            dma((chunks, 6)),
            dma((chunks, 6)),
            dma((chunks, group - 1)),
            dma((chunks, group - 1)),
            dma((chunks,)),
            dma,
        ],
        compiler_params=pltpu.CompilerParams(
            collective_id=0, has_side_effects=True, vmem_limit_bytes=60 * 1024 * 1024
        ),
    )(depth_offset, band_width, frames, edge_level)


def solution(mesh):
    placed = (P("scan", None, "col"), P(), P(), P(None, "col"))
    return jax.shard_map(
        body, mesh=mesh, in_specs=placed, out_specs=P("scan", None, "col"), check_vma=False
    )
```
